32 devices in a mesh: layer: 4 (over y, x), row: 4 (over z), col: 2 (over core).
Axes of the slice: x: 2, y: 2, z: 4, core: 2. Of those that a mesh axis runs over, the one named last changes fastest.
Arguments:
- statistic: float32 [8, 7168, 7168], P('layer', 'row', 'col'), as said below
- eigenbasis: float32 [8, 7168, 1024], P('layer', 'col'), may hold values from -0.0625 to 0.0625
Outputs:
- refreshed: float32 [8, 7168, 1024], P('layer', ('row', 'col'))
The draws below stay inside these ranges and needn't reach their ends.
Inputs may be any that keep to these rules, and one draw needn't show every extreme that they name: `statistic`: each layer's matrix is symmetric and positive definite.
All inputs are finite; a program needn't handle non-finite values.
Results may differ from the reference program's by a relative error of at most 0.00014.
Values sent between devices are 32-bit elements; how exact they have to be, the bound alone decides.
A program may use at most 192 MiB of HBM per device.

```python
import math
import jax
import jax.numpy as jnp
from jax import lax

D = 7168
K = 1024
LAYERS = 8


def draw_statistic(key, part):
    noise_key = jax.random.fold_in(key, 11)
    diag_key = jax.random.fold_in(key, 12)
    noise_part = jax.random.normal(noise_key, (LAYERS, D, D), jnp.float32) * (0.35 / math.sqrt(D))
    symmetric = (noise_part + jnp.swapaxes(noise_part, 1, 2)) * math.sqrt(0.5)
    upper_log = math.log(3.0)
    diag_values = jnp.exp(jax.random.uniform(diag_key, (LAYERS, D), jnp.float32, 0.0, upper_log))
    return symmetric + diag_values[:, :, None] * jnp.eye(D, dtype=jnp.float32)


def levels(rng, shape, cuts, smallest, top_value):
    gain, own = 1.0, jax.random.fold_in(rng, 6)
    for axis_at, parts in cuts:
        steps = jnp.exp(jax.random.uniform(jax.random.fold_in(own, axis_at), (parts,), jnp.float32, smallest / len(cuts), top_value / len(cuts)))
        gain = gain * jnp.repeat(steps, shape[axis_at] // parts).reshape([-1 if axis == axis_at else 1 for axis in range(len(shape))])
    return gain


def bell_draw(own_key, dims, width, most, shards=(), kind=jnp.bfloat16):
    loudness = levels(own_key, dims, shards, -0.22, 0.18) if shards else 1.0
    array = jax.random.normal(own_key, dims, jnp.float32) * width * loudness
    return jnp.minimum(jnp.maximum(array, -most), most).astype(kind)


def setup_inputs(seed: int = 0) -> dict:
    streams_of = jax.random.split(jax.random.key(seed), 3)
    statistic = draw_statistic(jax.random.fold_in(streams_of[2], 71), 0)
    eigenbasis = bell_draw(streams_of[1], (LAYERS, D, K), D ** -0.5, 0.0625, ((0, 4), (1, 2)), jnp.float32)
    return dict(statistic=statistic, eigenbasis=eigenbasis)


def refresh_layer(operands):
    stat_layer, basis_layer = operands
    product = jnp.dot(stat_layer.astype(jnp.float32), basis_layer.astype(jnp.float32), precision=lax.Precision.HIGHEST, preferred_element_type=jnp.float32)
    gram_matrix = lax.dot_general(product.astype(jnp.float32), product.astype(jnp.float32), (((0,), (0,)), ((), ())), precision=lax.Precision.HIGHEST, preferred_element_type=jnp.float32)
    factor = jnp.linalg.cholesky(gram_matrix)
    return lax.linalg.triangular_solve(factor, product, left_side=False, lower=True, transpose_a=True)

def reference(statistic, eigenbasis):
    return lax.map(refresh_layer, (statistic, eigenbasis))
```

```python
import jax
import jax.numpy as jnp
from jax import lax
from jax.experimental import pallas as pl
from jax.experimental.pallas import tpu as pltpu
from jax.sharding import PartitionSpec as P

B = 128
S = 8


def dot(left, right, dims):
    return lax.dot_general(
        left,
        right,
        (dims, ((), ())),
        precision=lax.Precision.HIGHEST,
        preferred_element_type=jnp.float32,
    )


def high(left, right, dims):
    return lax.dot_general(
        left,
        right,
        (dims, ((), ())),
        precision=lax.Precision.HIGH,
        preferred_element_type=jnp.float32,
    )


def invert_block(block):
    slabs = [block[S * g : S * (g + 1), :] for g in range(B // S)]
    lane = lax.broadcasted_iota(jnp.int32, (S, B), 1)
    sub = lax.broadcasted_iota(jnp.int32, (S, B), 0)
    for j in range(B):
        g, r = divmod(j, S)
        at_j = lane == j
        row = slabs[g][r : r + 1, :]
        scale = lax.rsqrt(jnp.broadcast_to(row[:, j : j + 1], (S, B)))
        done = jnp.where(at_j, 1.0, jnp.broadcast_to(row, (S, B))) * scale
        for h in range(g, B // S):
            slab = slabs[h]
            weight = jnp.broadcast_to(slab[:, j : j + 1], (S, B)) * scale
            new = jnp.where(at_j, 0.0, slab) - weight * done
            if h == g:
                new = jnp.where(sub > r, new, jnp.where(sub == r, done, slab))
            slabs[h] = new
    full = jnp.concatenate(slabs, axis=0)
    rows = lax.broadcasted_iota(jnp.int32, (B, B), 0)
    cols = lax.broadcasted_iota(jnp.int32, (B, B), 1)
    return jnp.where(cols <= rows, full, 0.0)


def inverse_kernel(gram_ref, out_ref, work, panel):
    size = gram_ref.shape[-1]
    blocks = size // B
    work[...] = gram_ref[0]
    col = lax.broadcasted_iota(jnp.int32, (B, size), 1)

    @pl.loop(0, blocks)
    def _(k):
        start = pl.multiple_of(k * B, B)
        here = pl.ds(start, B)
        inverse = invert_block(work[here, here])
        panel[...] = dot(inverse, work[here, :], ((1,), (0,)))
        panel[:, here] = inverse
        out_ref[0, here, :] = jnp.where(col < start + B, panel[...], 0.0)

        @pl.loop(k + 1, blocks)
        def _(i):
            rows = pl.ds(pl.multiple_of(i * B, B), B)
            work[rows, here] = jnp.zeros((B, B), jnp.float32)
            work[rows, :] -= dot(panel[:, rows], panel[...], ((0,), (0,)))


def inverse_factor(grams):
    count, size, _ = grams.shape
    spec = pl.BlockSpec((1, size, size), lambda m: (m, 0, 0))
    return pl.pallas_call(
        inverse_kernel,
        grid=(count,),
        out_shape=jax.ShapeDtypeStruct(grams.shape, jnp.float32),
        in_specs=[spec],
        out_specs=spec,
        scratch_shapes=[
            pltpu.VMEM((size, size), jnp.float32),
            pltpu.VMEM((B, size), jnp.float32),
        ],
        compiler_params=pltpu.CompilerParams(vmem_limit_bytes=40 * 2**20),
        cost_estimate=pl.CostEstimate(
            flops=count * size**3 * 12,
            bytes_accessed=count * size * size * 8,
            transcendentals=0,
        ),
    )(grams)


def on_device(statistic, eigenbasis):
    members = statistic.shape[0]
    cores = lax.axis_size("col")
    products, grams = [], []
    for member in range(members):
        product = lax.psum_scatter(
            high(statistic[member], eigenbasis[member], ((1,), (0,))),
            "col",
            scatter_dimension=0,
            tiled=True,
        )
        products.append(product)
        grams.append(high(product, product, ((0,), (0,))))
    grams = jnp.stack(grams)
    shared = members % cores == 0
    if shared:
        grams = lax.psum_scatter(grams, "col", scatter_dimension=0, tiled=True)
        grams = lax.psum(grams, "row")
    else:
        grams = lax.psum(grams, ("row", "col"))
    inverses = inverse_factor(grams)
    if shared:
        inverses = lax.all_gather(inverses, "col", axis=0, tiled=True)
    return jnp.stack(
        [high(products[m], inverses[m], ((1,), (1,))) for m in range(members)]
    )


def solution(mesh):
    placed = (P("layer", "row", "col"), P("layer", "col", None))
    return jax.shard_map(
        on_device,
        mesh=mesh,
        in_specs=placed,
        out_specs=P("layer", ("row", "col"), None),
        check_vma=False,
    )
```
